32 devices in a mesh: groups: 2 (over x), blk: 8 (over z, y), dp: 2 (over core).
Axes of the slice: x: 2, y: 2, z: 4, core: 2. Of those that a mesh axis runs over, the one named last changes fastest.
Arguments:
- particles: bfloat16 [32768, 4096], P(('groups', 'blk', 'dp')), parts along dimension 0, may hold values from -44 to 44
- defocus: int32 [32768], P(('groups', 'blk', 'dp')), parts along dimension 0, may hold values from 0 to 15
- pick_dest: int32 [32768, 1], P(('groups', 'blk', 'dp')), parts along dimension 0, may hold values from 0 to 15; in each aligned block of 1024 rows (0 to 1023, 1024 to 2047, ...) at most 128 rows name the same one
- references: bfloat16 [192, 4096], P(('groups', 'blk')), parts along dimension 0, may hold values from -4 to 4
- ctf_table: float32 [32, 4096], P('groups'), parts along dimension 0, may hold values from 0.1 to 1
Outputs:
- weighted_sums: float32 [192, 4096], P(('groups', 'blk', 'dp')), parts along dimension 0
- ctf_weights: float32 [192, 4096], P(('groups', 'blk', 'dp')), parts along dimension 0
- posterior: float32 [65536, 96], P(('groups', 'blk', 'dp')), parts along dimension 0
The draws below stay inside these ranges and needn't reach their ends.
There are 2 independent parts, one for each index of `groups`. The reference program is written for one: setup_inputs(seed, part) draws one part's arguments, and reference() takes and returns one part's arrays. A program takes and returns all parts, laid end to end along the dimension named above; each array names one. Nothing has to cross between parts.
Inputs may be any that keep to these rules, and one draw needn't show every extreme that they name: `pick_dest`: of the particles that one device holds, at most 128 name any one destination, and in every draw some device sends exactly 128 to one destination.
All inputs are finite; a program needn't handle non-finite values.
Results may differ from the reference program's by a relative error of at most 0.0028.
Values may be sent and summed in bfloat16 or wider, within the bound.
A program may use at most 128 MiB of HBM per device.

```python
import math
import jax
import jax.numpy as jnp
import numpy as np
from jax import lax

PIX = 4096
NDEF = 16
SRC = 1024
DEVS = 16
KR = 96
CAPP = 128
RECV = 2048
TOTAL = 16384
N_BLK = 8
N_DP = 2


def pieces(key):
    return jax.random.split(jax.random.fold_in(key, 91), 8)


def make_refs(key_list):
    ref_rows = jnp.clip(jax.random.normal(key_list[0], (KR, PIX), jnp.float32), -4.0, 4.0)
    return ref_rows


def make_ctf(key_list):
    return jax.random.uniform(key_list[1], (NDEF, PIX), jnp.float32, minval=0.1, maxval=1.0)


def make_defocus(key_list):
    return jax.random.randint(key_list[2], (TOTAL,), 0, NDEF, dtype=jnp.int32)


def draw_references(key, part):
    return make_refs(pieces(key)).astype(jnp.bfloat16)


def draw_ctf_table(key, part):
    return make_ctf(pieces(key))


def draw_defocus(key, part):
    return make_defocus(pieces(key))


def draw_particles(key, part):
    key_list = pieces(key)
    ref_rows = make_refs(key_list)
    ctf_rows = make_ctf(key_list)[make_defocus(key_list)]
    true_class = jax.random.randint(key_list[3], (TOTAL,), 0, KR, dtype=jnp.int32)
    signal = 0.1 * ctf_rows * ref_rows[true_class]
    noise_term = jnp.clip(jax.random.normal(key_list[4], (TOTAL, PIX), jnp.float32), -5.0, 5.0)
    drawn = signal + noise_term
    return jnp.clip(drawn, -44.0, 44.0).astype(jnp.bfloat16)


def deal_out(own_key, own, number, rows, number_of, top, reach, skew):
    sequence = jax.random.permutation(own_key, number_of)
    packed, usual = load_shares(number_of, rows * top, reach, skew, True), load_shares(number_of, rows * top, reach, skew, False)
    places = jnp.arange(number_of)

    def named(lengths, turn):
        used = int((lengths > 0).sum())
        fixed = max(1, used // 4)
        passed = fixed + (places - fixed + turn * (used - fixed)) % max(1, number_of - fixed)
        return jnp.zeros((number_of,), jnp.int32).at[sequence[jnp.where(places < fixed, places, passed)]].set(jnp.asarray(lengths, jnp.int32))

    lengths = jnp.where(number % 4 == 0, named(packed, number // 4), named(usual, number - number // 4 - 1))
    mixed = jax.random.permutation(jax.random.fold_in(own, 3), number_of)
    source_of, receiver = mixed[0:number_of // 2 * 2:2], mixed[1:number_of // 2 * 2:2]
    room = jnp.minimum(lengths[source_of] - 1, reach - lengths[receiver]) // 2
    room = jnp.where((source_of == sequence[0]) | (receiver == sequence[0]) | (lengths[receiver] == 0), 0, jnp.maximum(room, 0))
    passed = jax.random.randint(jax.random.fold_in(own, 4), (number_of // 2,), 0, 1 << 20) % (room + 1)
    lengths = lengths.at[source_of].add(-passed).at[receiver].add(passed)
    labels = jnp.searchsorted(jnp.cumsum(lengths), jnp.arange(rows * top), side="right").astype(jnp.int32)
    grid = labels.reshape(top, rows).T
    grid = grid[jax.random.permutation(jax.random.fold_in(own, 1), rows)]
    turn = jax.random.randint(jax.random.fold_in(own, 2), (rows, 1), 0, top)
    return jnp.take_along_axis(grid, (jnp.arange(top)[None, :] + turn) % top, axis=1)


def load_shares(amount, total, most, slope, full):
    weights = [(1 << 20) // math.isqrt(grade ** slope) + 1 for grade in range(1, amount + 1)]
    largest = most if full else min(most, max(-(-total // amount), total * weights[0] // sum(weights)))
    least = 1 if total - largest >= amount - 1 else 0
    holding, surplus = [largest] + [least] * (amount - 1), total - largest - least * (amount - 1)
    while surplus > 0:
        candidates = [i for i in range(1, amount) if holding[i] < largest] or [i for i in range(1, amount) if holding[i] < most]
        whole, budget = sum([weights[i] for i in candidates]), surplus
        for i in candidates:
            extra = min(most - holding[i], max(1, budget * weights[i] // whole), surplus)
            holding[i] = holding[i] + extra
            surplus = surplus - extra
    return np.array(holding)


def setup_inputs(seed: int = 0, part: int = 0) -> dict:
    key_of = jax.random.split(jax.random.key(seed), 6)
    own_keys = jax.random.split(jax.random.fold_in(key_of[5], part), 6)
    particles = draw_particles(jax.random.fold_in(jax.random.fold_in(key_of[5], part), 71), part)
    defocus = draw_defocus(jax.random.fold_in(jax.random.fold_in(key_of[5], part), 71), part)
    pick_dest_keys = jax.random.split(jax.random.fold_in(own_keys[2], 1), TOTAL // SRC)
    pick_dest_turns = jax.random.permutation(jax.random.fold_in(own_keys[2], 3), TOTAL // SRC)
    pick_dest = jax.vmap(lambda own, number: deal_out(jax.random.fold_in(own_keys[2], 2), own, number, SRC, DEVS, 1, CAPP, 2))(pick_dest_keys, pick_dest_turns).reshape((TOTAL, 1))
    references = draw_references(jax.random.fold_in(jax.random.fold_in(key_of[5], part), 71), part)
    ctf_table = draw_ctf_table(jax.random.fold_in(jax.random.fold_in(key_of[5], part), 71), part)
    return dict(particles=particles, defocus=defocus, pick_dest=pick_dest, references=references, ctf_table=ctf_table)


def reference(particles, defocus, pick_dest, references, ctf_table):
    score_scale = 1.0 / math.sqrt(PIX)
    modulation = ctf_table[defocus]
    modulated = (particles.astype(jnp.float32) * modulation).astype(jnp.bfloat16)
    ctf_square = ctf_table * ctf_table
    ref_float = references.astype(jnp.float32)
    quadratic = 0.5 * jnp.dot(ctf_square, (ref_float * ref_float).T, precision=lax.Precision.HIGHEST)
    cross_term = jnp.dot(modulated, references.T, preferred_element_type=jnp.float32)
    scores = score_scale * (cross_term - quadratic[defocus])
    largest = lax.optimization_barrier(jnp.max(scores, axis=1, keepdims=True))
    exponent = jnp.exp(scores - largest)
    weights = exponent / lax.optimization_barrier(jnp.sum(exponent, axis=1, keepdims=True))
    weights_low = weights.astype(jnp.bfloat16)
    weighted_sums = jnp.dot(weights_low.T, modulated, preferred_element_type=jnp.float32)
    onehot = (defocus[:, None] == jnp.arange(NDEF, dtype=jnp.int32)[None, :]).astype(jnp.float32)
    class_sums = jnp.dot(onehot.T, weights, precision=lax.Precision.HIGHEST)
    ctf_weights = jnp.dot(class_sums.T, ctf_square, precision=lax.Precision.HIGHEST)
    device_count = N_BLK * N_DP
    dest_grid = pick_dest[:, 0].reshape(device_count, SRC)
    dest_hot = (dest_grid[:, :, None] == jnp.arange(device_count, dtype=jnp.int32)[None, None, :]).astype(jnp.int32)
    earlier = jnp.cumsum(dest_hot, axis=1) - dest_hot
    ranking = lax.optimization_barrier(jnp.sum(earlier * dest_hot, axis=2))
    source_ids = jnp.arange(device_count, dtype=jnp.int32)[:, None]
    out_row = (dest_grid * RECV + source_ids * CAPP + ranking).reshape(-1).astype(jnp.int32)
    posterior = jnp.zeros((device_count * RECV, KR), jnp.float32).at[out_row].set(weights)
    return (weighted_sums, ctf_weights, posterior)
```

```python
import functools
import math

import jax
import jax.numpy as jnp
from jax import lax
from jax.experimental import pallas as pl
from jax.experimental.pallas import tpu as pltpu
from jax.sharding import PartitionSpec as P

MESH = pl.DeviceIdType.MESH
BF = jnp.bfloat16
F32 = jnp.float32
PAD = 16
LANES = 128
ROWS = 128
COLS = 512
SCORE_ROWS = 256


def dot_nt(left, right, **kw):
    return lax.dot_general(
        left, right, (((1,), (1,)), ((), ())), preferred_element_type=F32, **kw
    )


def dot_nn(left, right, **kw):
    return lax.dot_general(
        left, right, (((1,), (0,)), ((), ())), preferred_element_type=F32, **kw
    )


def split3(value):
    high = value.astype(BF)
    rest = value - high.astype(F32)
    middle = rest.astype(BF)
    low = (rest - middle.astype(F32)).astype(BF)
    return high, middle, low


def kernel(
    n_blk, n_dp, own_rows, capacity,
    particles, defocus, dest, refs_in, ctf_in,
    sums_out, ctf_out, post_out,
    part, refs, table, square, onehot_t, onehot, slots, weights, low,
    kept, mate_send, mate_recv, chip_send, chip_recv, class_send, class_recv,
    final_send, final_recv, cfinal_send, cfinal_recv, post_send, post_recv,
    part_sem, ref_ssem, ref_rsem, fwd_ssem, fwd_rsem, post_ssem, post_rsem,
    mate_ssem, mate_rsem, chip_ssem, chip_rsem, class_ssem, class_rsem,
    final_ssem, final_rsem,
):
    held, pix = part.shape
    mod = part
    half = pix // n_dp
    devices = n_blk * n_dp
    padded = n_blk * PAD
    kinds = ctf_in.shape[0]
    rows_mine = own_rows // n_dp
    score_scale = 1.0 / math.sqrt(pix)
    blk = lax.axis_index("blk")
    core = lax.axis_index("dp")
    me = blk * n_dp + core
    mate = {"dp": 1 - core}
    my_cols = pl.ds(pl.multiple_of(core * half, half), half)
    mate_cols = pl.ds(pl.multiple_of((1 - core) * half, half), half)

    loads = []
    for chunk in range(held // ROWS):
        copy = pltpu.make_async_copy(
            particles.at[pl.ds(chunk * ROWS, ROWS)],
            part.at[pl.ds(chunk * ROWS, ROWS)],
            part_sem.at[chunk],
        )
        copy.start()
        loads.append(copy)

    barrier = pltpu.get_barrier_semaphore()
    for step in range(1, devices):
        other = lax.rem(me + step, devices)
        pl.semaphore_signal(
            barrier, inc=1, device_id={"blk": other // n_dp, "dp": lax.rem(other, n_dp)},
            device_id_type=MESH,
        )
    refs[blk, 0:own_rows, :] = refs_in[...]
    zeros = jnp.zeros((PAD - own_rows, pix), BF)
    refs[blk, own_rows:PAD, :] = zeros
    pl.semaphore_wait(barrier, devices - 1)

    ref_copies = []
    for step in range(1, n_blk):
        target = lax.rem(blk + step, n_blk)
        piece = refs.at[blk, :, my_cols]
        copy = pltpu.make_async_remote_copy(
            src_ref=piece, dst_ref=piece,
            send_sem=ref_ssem.at[step], recv_sem=ref_rsem.at[step],
            device_id={"blk": target}, device_id_type=MESH,
        )
        copy.start()
        ref_copies.append(copy)

    kind_rows = lax.broadcasted_iota(jnp.int32, (LANES, held), 0)
    class_row = defocus[...]
    hot = jnp.where(
        (lax.rem(kind_rows, kinds) == class_row) & (kind_rows < 3 * kinds), 1.0, 0.0
    ).astype(F32)
    onehot_t[...] = hot
    onehot[...] = hot.T.astype(BF)
    table[...] = jnp.zeros_like(table)
    square[...] = jnp.zeros_like(square)
    ctf = ctf_in[...]
    for index, value in enumerate(split3(ctf)):
        table[index * kinds:(index + 1) * kinds, :] = value
    for index, value in enumerate(split3(ctf * ctf)):
        square[index * kinds:(index + 1) * kinds, :] = value

    forwards = []

    def forward(step):
        ref_copies[step - 1].wait_recv()
        source = lax.rem(blk + n_blk - step, n_blk)
        piece = refs.at[source, :, my_cols]
        copy = pltpu.make_async_remote_copy(
            src_ref=piece, dst_ref=piece,
            send_sem=fwd_ssem.at[step], recv_sem=fwd_rsem.at[step],
            device_id=mate, device_id_type=MESH,
        )
        copy.start()
        forwards.append(copy)

    pending = list(range(1, n_blk))
    per_chunk = -(-(n_blk - 1) // (held // ROWS))
    for chunk in range(held // ROWS):
        loads[chunk].wait()
        base = chunk * ROWS
        chosen = onehot[base:base + ROWS, :]

        def modulate(block, carry):
            columns = pl.ds(pl.multiple_of(block * COLS, COLS), COLS)
            factor = dot_nn(chosen, table[:, columns])
            mod[base:base + ROWS, columns] = (
                part[base:base + ROWS, columns].astype(F32) * factor
            ).astype(BF)
            return carry

        lax.fori_loop(0, pix // COLS, modulate, 0)
        for _ in range(per_chunk):
            if pending and chunk > 0 or len(pending) > held // ROWS:
                forward(pending.pop(0))
    while pending:
        forward(pending.pop(0))

    dest_row = dest[...]
    dest_hot = jnp.where(
        lax.broadcasted_iota(jnp.int32, (devices, held), 0) == dest_row, 1.0, 0.0
    ).astype(F32)
    before = jnp.where(
        lax.broadcasted_iota(jnp.int32, (held, held), 0)
        < lax.broadcasted_iota(jnp.int32, (held, held), 1), 1.0, 0.0
    ).astype(BF)
    earlier = dot_nn(dest_hot.astype(BF), before)
    rank = jnp.sum(earlier * dest_hot, axis=0, keepdims=True)
    slots[...] = dest_row.astype(F32) * float(capacity) + rank

    for copy in forwards:
        copy.wait_recv()

    def gather_square(block, total):
        columns = pl.ds(pl.multiple_of(block * COLS, COLS), COLS)
        value = refs[:, :, columns].reshape(padded, COLS).astype(F32)
        value = value * value
        high = value.astype(BF)
        rest = (value - high.astype(F32)).astype(BF)
        factor = square[:, columns]
        return total + dot_nt(high, factor) + dot_nt(rest, factor)

    quadratic = 0.5 * lax.fori_loop(
        0, pix // COLS, gather_square, jnp.zeros((padded, LANES), F32)
    )
    valid = lax.rem(lax.broadcasted_iota(jnp.int32, (padded, SCORE_ROWS), 0), PAD) < own_rows
    every_ref = refs[...].reshape(padded, pix)
    for chunk in range(held // SCORE_ROWS):
        span = slice(chunk * SCORE_ROWS, (chunk + 1) * SCORE_ROWS)
        cross = dot_nt(every_ref, mod[span, :])
        offset = dot_nn(quadratic, onehot_t[:, span], precision=lax.Precision.HIGHEST)
        scores = jnp.where(valid, (cross - offset) * score_scale, -1e30)
        largest = jnp.max(scores, axis=0, keepdims=True)
        exponent = jnp.exp(scores - largest)
        share = exponent * (1.0 / jnp.sum(exponent, axis=0, keepdims=True))
        weights[:, span] = share
        low[:, span] = share.astype(BF)

    mate_copies = []
    for block in range(half // COLS):
        source = pl.ds(pl.multiple_of((1 - core) * half + block * COLS, COLS), COLS)
        local = pl.ds(block * COLS, COLS)
        mate_send[:, :, local] = dot_nn(low[...], mod[:, source]).reshape(
            n_blk, PAD, COLS).astype(BF)
        copy = pltpu.make_async_remote_copy(
            src_ref=mate_send.at[:, :, local], dst_ref=mate_recv.at[:, :, local],
            send_sem=mate_ssem.at[block], recv_sem=mate_rsem.at[block],
            device_id=mate, device_id_type=MESH,
        )
        copy.start()
        mate_copies.append(copy)
    for block in range(half // COLS):
        source = pl.ds(pl.multiple_of(core * half + block * COLS, COLS), COLS)
        local = pl.ds(block * COLS, COLS)
        kept[:, :, local] = dot_nn(low[...], mod[:, source]).reshape(n_blk, PAD, COLS)
    class_send[...] = dot_nt(
        weights[...], onehot_t[...], precision=lax.Precision.HIGHEST
    ).reshape(n_blk, PAD, LANES)
    chip_copies = []
    for step in range(1, n_blk):
        target = lax.rem(blk + step, n_blk)
        copy = pltpu.make_async_remote_copy(
            src_ref=class_send.at[target], dst_ref=class_recv.at[step],
            send_sem=class_ssem.at[step], recv_sem=class_rsem.at[step],
            device_id={"blk": target}, device_id_type=MESH,
        )
        copy.start()
        chip_copies.append(copy)
    for block, copy in enumerate(mate_copies):
        copy.wait_recv()
        local = pl.ds(block * COLS, COLS)
        both = kept[:, :, local] + mate_recv[:, :, local].astype(F32)
        kept[:, :, local] = both
        chip_send[:, :, local] = both.astype(BF)
    for step in range(1, n_blk):
        target = lax.rem(blk + step, n_blk)
        copy = pltpu.make_async_remote_copy(
            src_ref=chip_send.at[target],
            dst_ref=chip_recv.at[step],
            send_sem=chip_ssem.at[step], recv_sem=chip_rsem.at[step],
            device_id={"blk": target}, device_id_type=MESH,
        )
        copy.start()
        chip_copies.append(copy)

    kept_refs = n_blk * own_rows
    pick_row = lax.broadcasted_iota(jnp.int32, (kept_refs, padded), 0)
    pick = jnp.where(
        (pick_row // own_rows) * PAD + lax.rem(pick_row, own_rows)
        == lax.broadcasted_iota(jnp.int32, (kept_refs, padded), 1), 1.0, 0.0
    ).astype(BF)
    compact = dot_nn(pick, low[...]).astype(BF)
    slot_row = slots[...]
    place = lax.broadcasted_iota(jnp.int32, (capacity, held), 0)
    post_copies = []
    for step in list(range(1, devices)) + [0]:
        other = lax.rem(me + step, devices)
        chosen = jnp.where(
            (place + other * capacity).astype(F32) == slot_row, 1.0, 0.0
        ).astype(BF)
        block = dot_nt(compact, chosen)
        if step == 0:
            post_recv[0] = block.astype(BF)
        else:
            post_send[step] = block.astype(BF)
            copy = pltpu.make_async_remote_copy(
                src_ref=post_send.at[step], dst_ref=post_recv.at[step],
                send_sem=post_ssem.at[step], recv_sem=post_rsem.at[step],
                device_id={"blk": other // n_dp, "dp": lax.rem(other, n_dp)},
                device_id_type=MESH,
            )
            copy.start()
            post_copies.append(copy)

    total = kept[blk]
    classes = class_send[blk]
    for copy in chip_copies:
        copy.wait_recv()
    for step in range(1, n_blk):
        total = total + chip_recv[step].astype(F32)
        classes = classes + class_recv[step]
    first, second = total[0:rows_mine], total[rows_mine:own_rows]
    final_send[0:rows_mine, :] = jnp.where(core == 0, second, first)
    cfinal_send[...] = classes
    finals = []
    for source, target, index in ((final_send, final_recv, 0), (cfinal_send, cfinal_recv, 1)):
        copy = pltpu.make_async_remote_copy(
            src_ref=source, dst_ref=target,
            send_sem=final_ssem.at[index], recv_sem=final_rsem.at[index],
            device_id=mate, device_id_type=MESH,
        )
        copy.start()
        finals.append(copy)
    sums_out[:, my_cols] = jnp.where(core == 0, first, second)

    for step in [0] + list(range(1, devices)):
        if step:
            post_copies[step - 1].wait_recv()
    for source in range(devices):
        step = lax.rem(me + devices - source, devices)
        post_out[:, source * capacity:(source + 1) * capacity] = post_recv[step].astype(F32)

    for copy in finals:
        copy.wait_recv()
    sums_out[:, mate_cols] = final_recv[0:rows_mine, :]
    classes = classes + cfinal_recv[...]
    mine = jnp.where(core == 0, classes[0:rows_mine], classes[rows_mine:own_rows])
    mine = mine[:, 0:kinds]

    ctf_out[...] = dot_nn(
        mine, ctf_in[...] * ctf_in[...], precision=lax.Precision.HIGHEST
    )

    for copy in ref_copies + forwards + mate_copies + chip_copies + post_copies + finals:
        copy.wait_send()


def per_device(particles, defocus, pick_dest, references, ctf_table):
    held, pix = particles.shape
    own_rows = references.shape[0]
    n_blk, n_dp = lax.axis_size("blk"), lax.axis_size("dp")
    devices = n_blk * n_dp
    capacity = max(2, 2 * held // devices)
    kept_refs = n_blk * own_rows
    padded = n_blk * PAD
    half = pix // n_dp
    rows_mine = own_rows // n_dp
    vmem = pl.BlockSpec(memory_space=pltpu.VMEM)
    dma = pltpu.SemaphoreType.DMA
    sums, weights, posterior = pl.pallas_call(
        functools.partial(kernel, n_blk, n_dp, own_rows, capacity),
        out_shape=(
            jax.ShapeDtypeStruct((rows_mine, pix), F32),
            jax.ShapeDtypeStruct((rows_mine, pix), F32),
            jax.ShapeDtypeStruct((kept_refs, devices * capacity), F32),
        ),
        in_specs=[pl.BlockSpec(memory_space=pl.ANY), vmem, vmem, vmem, vmem],
        out_specs=(vmem, vmem, vmem),
        scratch_shapes=[
            pltpu.VMEM((held, pix), BF),
            pltpu.VMEM((n_blk, PAD, pix), BF),
            pltpu.VMEM((LANES, pix), BF),
            pltpu.VMEM((LANES, pix), BF),
            pltpu.VMEM((LANES, held), F32),
            pltpu.VMEM((held, LANES), BF),
            pltpu.VMEM((1, held), F32),
            pltpu.VMEM((padded, held), F32),
            pltpu.VMEM((padded, held), BF),
            pltpu.VMEM((n_blk, PAD, half), F32),
            pltpu.VMEM((n_blk, PAD, half), BF),
            pltpu.VMEM((n_blk, PAD, half), BF),
            pltpu.VMEM((n_blk, PAD, half), BF),
            pltpu.VMEM((n_blk, PAD, half), BF),
            pltpu.VMEM((n_blk, PAD, LANES), F32),
            pltpu.VMEM((n_blk, PAD, LANES), F32),
            pltpu.VMEM((8, half), F32),
            pltpu.VMEM((8, half), F32),
            pltpu.VMEM((PAD, LANES), F32),
            pltpu.VMEM((PAD, LANES), F32),
            pltpu.VMEM((devices, kept_refs, capacity), BF),
            pltpu.VMEM((devices, kept_refs, capacity), BF),
            dma((held // ROWS,)),
            dma((n_blk,)), dma((n_blk,)), dma((n_blk,)), dma((n_blk,)),
            dma((devices,)), dma((devices,)),
            dma((half // COLS,)), dma((half // COLS,)),
            dma((n_blk,)), dma((n_blk,)), dma((n_blk,)), dma((n_blk,)),
            dma((2,)), dma((2,)),
        ],
        compiler_params=pltpu.CompilerParams(
            collective_id=0, has_side_effects=True, vmem_limit_bytes=60 << 20
        ),
        name="em_step",
    )(
        particles,
        defocus.reshape(1, held),
        pick_dest.reshape(1, held),
        references,
        ctf_table,
    )
    return sums, weights, posterior.T


def solution(mesh):
    placed = (
        P(("groups", "blk", "dp"), None),
        P(("groups", "blk", "dp")),
        P(("groups", "blk", "dp"), None),
        P(("groups", "blk"), None),
        P("groups", None),
    )
    return jax.shard_map(
        per_device,
        mesh=mesh,
        in_specs=placed,
        out_specs=(
            P(("groups", "blk", "dp"), None),
            P(("groups", "blk", "dp"), None),
            P(("groups", "blk", "dp"), None),
        ),
        check_vma=False,
    )
```

```python
import functools
import math

import jax
import jax.numpy as jnp
from jax import lax
from jax.experimental import pallas as pl
from jax.experimental.pallas import tpu as pltpu
from jax.sharding import PartitionSpec as P

MESH = pl.DeviceIdType.MESH
BF = jnp.bfloat16
F32 = jnp.float32
PAD = 16
LANES = 128
ROWS = 256
TILE = 256
COLS = 512
SCORE_ROWS = 256


def dot_nt(left, right, **kw):
    return lax.dot_general(
        left, right, (((1,), (1,)), ((), ())), preferred_element_type=F32, **kw
    )


def dot_nn(left, right, **kw):
    return lax.dot_general(
        left, right, (((1,), (0,)), ((), ())), preferred_element_type=F32, **kw
    )


def split3(value):
    high = value.astype(BF)
    rest = value - high.astype(F32)
    middle = rest.astype(BF)
    low = (rest - middle.astype(F32)).astype(BF)
    return high, middle, low


def kernel(
    n_blk, n_dp, own_rows, capacity,
    particles, defocus, dest, refs_in, ctf_in,
    sums_out, class_out, post_recv,
    part, refs, table, square, onehot_t, onehot, slots, weights, low,
    kept, mate_send, mate_recv, side_send, side_recv, chip_send, chip_recv, class_send, class_recv,
    final_send, final_recv, cfinal_send, cfinal_recv, post_send,
    part_sem, ref_ssem, ref_rsem, near_ssem, near_rsem, fwd_ssem, fwd_rsem, post_ssem, post_rsem,
    mate_ssem, mate_rsem, side_ssem, side_rsem, chip_ssem, chip_rsem, class_ssem, class_rsem,
    final_ssem, final_rsem,
):
    held, pix = part.shape
    mod = part
    half = pix // n_dp
    devices = n_blk * n_dp
    padded = n_blk * PAD
    kinds = ctf_in.shape[0]
    rows_mine = own_rows // n_dp
    score_scale = 1.0 / math.sqrt(pix)
    blk = lax.axis_index("blk")
    near = 2
    deep = n_blk // near
    z, y = blk // near, lax.rem(blk, near)
    partner = {"blk": z * near + 1 - y}
    core = lax.axis_index("dp")
    me = blk * n_dp + core
    mate = {"dp": 1 - core}
    my_cols = pl.ds(pl.multiple_of(core * half, half), half)
    mate_cols = pl.ds(pl.multiple_of((1 - core) * half, half), half)

    loads = []
    for chunk in range(held // ROWS):
        copy = pltpu.make_async_copy(
            particles.at[pl.ds(chunk * ROWS, ROWS)],
            part.at[pl.ds(chunk * ROWS, ROWS)],
            part_sem.at[chunk],
        )
        copy.start()
        loads.append(copy)

    barrier = pltpu.get_barrier_semaphore()
    for step in range(1, devices):
        other = lax.rem(me + step, devices)
        pl.semaphore_signal(
            barrier, inc=1, device_id={"blk": other // n_dp, "dp": lax.rem(other, n_dp)},
            device_id_type=MESH,
        )
    refs[blk, 0:own_rows, :] = refs_in[...]
    zeros = jnp.zeros((PAD - own_rows, pix), BF)
    refs[blk, own_rows:PAD, :] = zeros
    kind_rows = lax.broadcasted_iota(jnp.int32, (LANES, held), 0)
    class_row = defocus[...]
    hot = jnp.where(
        (lax.rem(kind_rows, kinds) == class_row) & (kind_rows < 3 * kinds), 1.0, 0.0
    ).astype(F32)
    onehot_t[...] = hot
    onehot[...] = hot.T.astype(BF)
    table[...] = jnp.zeros_like(table)
    square[...] = jnp.zeros_like(square)
    ctf = ctf_in[...]
    for index, value in enumerate(split3(ctf)):
        table[index * kinds:(index + 1) * kinds, :] = value
    for index, value in enumerate(split3(ctf * ctf)):
        square[index * kinds:(index + 1) * kinds, :] = value

    pl.semaphore_wait(barrier, devices - 1)

    def send_ref(owner, send_sem, recv_sem, target):
        piece = refs.at[owner, :, my_cols]
        copy = pltpu.make_async_remote_copy(
            src_ref=piece, dst_ref=piece, send_sem=send_sem, recv_sem=recv_sem,
            device_id=target, device_id_type=MESH,
        )
        copy.start()
        return copy

    near_copies = [None] * deep
    far_copies = [None] * deep
    forwards = []
    for step in range(1, deep):
        far_copies[step] = send_ref(
            blk, ref_ssem.at[step], ref_rsem.at[step],
            {"blk": lax.rem(z + step, deep) * near + y},
        )
    near_copies[0] = send_ref(blk, near_ssem.at[0], near_rsem.at[0], partner)

    def forward_far(step):
        far_copies[step].wait_recv()
        owner = lax.rem(z + deep - step, deep) * near + y
        near_copies[step] = send_ref(owner, near_ssem.at[step], near_rsem.at[step], partner)
        forwards.append(send_ref(owner, fwd_ssem.at[step], fwd_rsem.at[step], mate))

    def forward_near(step):
        near_copies[step].wait_recv()
        owner = lax.rem(z + deep - step, deep) * near + 1 - y
        index = deep + step
        forwards.append(send_ref(owner, fwd_ssem.at[index], fwd_rsem.at[index], mate))

    order = sorted(range(1, deep), key=lambda step: min(step, deep - step))
    pending = [functools.partial(forward_far, step) for step in order]
    pending += [functools.partial(forward_near, step) for step in [0] + order]
    for chunk in range(held // ROWS):
        loads[chunk].wait()
        base = chunk * ROWS
        chosen = onehot[base:base + ROWS, :]

        for block in range(pix // TILE):
            columns = slice(block * TILE, (block + 1) * TILE)
            factor = dot_nn(chosen, table[:, columns])
            mod[base:base + ROWS, columns] = (
                part[base:base + ROWS, columns].astype(F32) * factor
            ).astype(BF)
        if chunk < deep - 1:
            pending.pop(0)()

    while pending:
        pending.pop(0)()

    dest_row = dest[...]
    dest_hot = jnp.where(
        lax.broadcasted_iota(jnp.int32, (devices, held), 0) == dest_row, 1.0, 0.0
    ).astype(F32)
    before = jnp.where(
        lax.broadcasted_iota(jnp.int32, (held, held), 0)
        < lax.broadcasted_iota(jnp.int32, (held, held), 1), 1.0, 0.0
    ).astype(BF)
    earlier = dot_nn(dest_hot.astype(BF), before)
    rank = jnp.sum(earlier * dest_hot, axis=0, keepdims=True)
    slots[...] = dest_row.astype(F32) * float(capacity) + rank

    for copy in forwards:
        copy.wait_recv()

    def gather_square(block, total):
        columns = pl.ds(pl.multiple_of(block * COLS, COLS), COLS)
        value = refs[:, :, columns].reshape(padded, COLS).astype(F32)
        value = value * value
        high = value.astype(BF)
        rest = (value - high.astype(F32)).astype(BF)
        factor = square[:, columns]
        return total + dot_nt(high, factor) + dot_nt(rest, factor)

    quadratic = 0.5 * lax.fori_loop(
        0, pix // COLS, gather_square, jnp.zeros((padded, LANES), F32), unroll=True
    )
    valid = lax.rem(lax.broadcasted_iota(jnp.int32, (padded, SCORE_ROWS), 0), PAD) < own_rows
    every_ref = refs[...].reshape(padded, pix)
    for chunk in range(held // SCORE_ROWS):
        span = slice(chunk * SCORE_ROWS, (chunk + 1) * SCORE_ROWS)
        cross = dot_nt(every_ref, mod[span, :])
        offset = dot_nn(quadratic, onehot_t[:, span], precision=lax.Precision.HIGHEST)
        scores = jnp.where(valid, (cross - offset) * score_scale, -1e30)
        largest = jnp.max(scores, axis=0, keepdims=True)
        exponent = jnp.exp(scores - largest)
        share = exponent * (1.0 / jnp.sum(exponent, axis=0, keepdims=True))
        weights[:, span] = share
        low[:, span] = share.astype(BF)

    mate_copies = []
    for block in range(half // COLS):
        source = pl.ds(pl.multiple_of((1 - core) * half + block * COLS, COLS), COLS)
        local = pl.ds(block * COLS, COLS)
        mate_send[:, :, local] = dot_nn(low[...], mod[:, source]).reshape(
            n_blk, PAD, COLS).astype(BF)
        copy = pltpu.make_async_remote_copy(
            src_ref=mate_send.at[:, :, local], dst_ref=mate_recv.at[:, :, local],
            send_sem=mate_ssem.at[block], recv_sem=mate_rsem.at[block],
            device_id=mate, device_id_type=MESH,
        )
        copy.start()
        mate_copies.append(copy)
    kept_refs = n_blk * own_rows
    pick_row = lax.broadcasted_iota(jnp.int32, (kept_refs, padded), 0)
    pick = jnp.where(
        (pick_row // own_rows) * PAD + lax.rem(pick_row, own_rows)
        == lax.broadcasted_iota(jnp.int32, (kept_refs, padded), 1), 1.0, 0.0
    ).astype(BF)
    compact = dot_nn(pick, low[...]).astype(BF)
    slot_row = slots[...]
    place = lax.broadcasted_iota(jnp.int32, (capacity, held), 0)
    post_copies = []
    for step in list(range(1, devices)) + [0]:
        other = lax.rem(me + step, devices)
        chosen = jnp.where(
            (place + other * capacity).astype(F32) == slot_row, 1.0, 0.0
        ).astype(BF)
        block = dot_nt(compact, chosen)
        post_send[step] = block.astype(BF)
        if step == 0:
            own_copy = pltpu.make_async_copy(
                post_send.at[0], post_recv.at[me], post_rsem.at[0]
            )
            own_copy.start()
        else:
            copy = pltpu.make_async_remote_copy(
                src_ref=post_send.at[step], dst_ref=post_recv.at[me],
                send_sem=post_ssem.at[step], recv_sem=post_rsem.at[step],
                device_id={"blk": other // n_dp, "dp": lax.rem(other, n_dp)},
                device_id_type=MESH,
            )
            copy.start()
            post_copies.append(copy)

    for block in range(half // COLS):
        source = pl.ds(pl.multiple_of(core * half + block * COLS, COLS), COLS)
        local = pl.ds(block * COLS, COLS)
        kept[:, :, local] = dot_nn(low[...], mod[:, source]).reshape(n_blk, PAD, COLS)
    class_send[...] = dot_nt(
        weights[...], onehot_t[...], precision=lax.Precision.HIGHEST
    ).reshape(n_blk, PAD, LANES)
    chip_copies = []
    for step in range(1, n_blk):
        target = lax.rem(blk + step, n_blk)
        copy = pltpu.make_async_remote_copy(
            src_ref=class_send.at[target], dst_ref=class_recv.at[step],
            send_sem=class_ssem.at[step], recv_sem=class_rsem.at[step],
            device_id={"blk": target}, device_id_type=MESH,
        )
        copy.start()
        chip_copies.append(copy)
    side_copies = []
    for block, copy in enumerate(mate_copies):
        copy.wait_recv()
        local = pl.ds(block * COLS, COLS)
        both = kept[:, :, local] + mate_recv[:, :, local].astype(F32)
        both = both.reshape(deep, near, PAD, COLS)
        kept[0:deep, :, local] = jnp.where(y == 0, both[:, 0], both[:, 1])
        side_send[:, :, local] = jnp.where(y == 0, both[:, 1], both[:, 0]).astype(BF)
        copy = pltpu.make_async_remote_copy(
            src_ref=side_send.at[:, :, local], dst_ref=side_recv.at[:, :, local],
            send_sem=side_ssem.at[block], recv_sem=side_rsem.at[block],
            device_id=partner, device_id_type=MESH,
        )
        copy.start()
        side_copies.append(copy)
    for block, copy in enumerate(side_copies):
        copy.wait_recv()
        local = pl.ds(block * COLS, COLS)
        both = kept[0:deep, :, local] + side_recv[:, :, local].astype(F32)
        kept[0:deep, :, local] = both
        chip_send[:, :, local] = both.astype(BF)
        for step in range(1, deep):
            target = lax.rem(z + step, deep)
            copy = pltpu.make_async_remote_copy(
                src_ref=chip_send.at[target, :, local],
                dst_ref=chip_recv.at[step, :, local],
                send_sem=chip_ssem.at[step, block], recv_sem=chip_rsem.at[step, block],
                device_id={"blk": target * near + y}, device_id_type=MESH,
            )
            copy.start()
            chip_copies.append(copy)

    total = kept[z]
    classes = class_send[blk]
    for copy in chip_copies:
        copy.wait_recv()
    for step in range(1, deep):
        total = total + chip_recv[step].astype(F32)
    for step in range(1, n_blk):
        classes = classes + class_recv[step]
    first, second = total[0:rows_mine], total[rows_mine:own_rows]
    final_send[0:rows_mine, :] = jnp.where(core == 0, second, first)
    cfinal_send[...] = classes
    finals = []
    for source, target, index in ((final_send, final_recv, 0), (cfinal_send, cfinal_recv, 1)):
        copy = pltpu.make_async_remote_copy(
            src_ref=source, dst_ref=target,
            send_sem=final_ssem.at[index], recv_sem=final_rsem.at[index],
            device_id=mate, device_id_type=MESH,
        )
        copy.start()
        finals.append(copy)
    sums_out[:, my_cols] = jnp.where(core == 0, first, second)

    for copy in finals:
        copy.wait_recv()
    sums_out[:, mate_cols] = final_recv[0:rows_mine, :]
    classes = classes + cfinal_recv[...]
    mine = jnp.where(core == 0, classes[0:rows_mine], classes[rows_mine:own_rows])
    class_out[0:rows_mine, :] = mine
    for copy in post_copies:
        copy.wait_recv()
    own_copy.wait()

    for copy in far_copies[1:] + near_copies + forwards + mate_copies + side_copies + chip_copies + post_copies + finals:
        copy.wait_send()


def finish(sums_in, class_in, ctf_in, post_in, sums_out, ctf_out, post_out):
    kinds = ctf_in.shape[0]
    rows_mine = sums_in.shape[0]
    capacity = post_in.shape[2]
    for source in range(post_in.shape[0]):
        post_out[:, source * capacity:(source + 1) * capacity] = post_in[source].astype(F32)
    sums_out[...] = sums_in[...]
    ctf = ctf_in[...]
    ctf_out[...] = dot_nn(
        class_in[0:rows_mine, 0:kinds], ctf * ctf, precision=lax.Precision.HIGHEST
    )


def per_device(particles, defocus, pick_dest, references, ctf_table):
    held, pix = particles.shape
    own_rows = references.shape[0]
    n_blk, n_dp = lax.axis_size("blk"), lax.axis_size("dp")
    devices = n_blk * n_dp
    capacity = max(2, 2 * held // devices)
    kept_refs = n_blk * own_rows
    padded = n_blk * PAD
    half = pix // n_dp
    rows_mine = own_rows // n_dp
    vmem = pl.BlockSpec(memory_space=pltpu.VMEM)
    dma = pltpu.SemaphoreType.DMA
    sums, classes, posterior = pl.pallas_call(
        functools.partial(kernel, n_blk, n_dp, own_rows, capacity),
        out_shape=(
            jax.ShapeDtypeStruct((rows_mine, pix), F32),
            jax.ShapeDtypeStruct((8, LANES), F32),
            jax.ShapeDtypeStruct((devices, kept_refs, capacity), BF),
        ),
        in_specs=[pl.BlockSpec(memory_space=pl.ANY), vmem, vmem, vmem, vmem],
        out_specs=(vmem, vmem, pl.BlockSpec(memory_space=pl.ANY)),
        scratch_shapes=[
            pltpu.VMEM((held, pix), BF),
            pltpu.VMEM((n_blk, PAD, pix), BF),
            pltpu.VMEM((LANES, pix), BF),
            pltpu.VMEM((LANES, pix), BF),
            pltpu.VMEM((LANES, held), F32),
            pltpu.VMEM((held, LANES), BF),
            pltpu.VMEM((1, held), F32),
            pltpu.VMEM((padded, held), F32),
            pltpu.VMEM((padded, held), BF),
            pltpu.VMEM((n_blk, PAD, half), F32),
            pltpu.VMEM((n_blk, PAD, half), BF),
            pltpu.VMEM((n_blk, PAD, half), BF),
            pltpu.VMEM((n_blk // 2, PAD, half), BF),
            pltpu.VMEM((n_blk // 2, PAD, half), BF),
            pltpu.VMEM((n_blk // 2, PAD, half), BF),
            pltpu.VMEM((n_blk // 2, PAD, half), BF),
            pltpu.VMEM((n_blk, PAD, LANES), F32),
            pltpu.VMEM((n_blk, PAD, LANES), F32),
            pltpu.VMEM((8, half), F32),
            pltpu.VMEM((8, half), F32),
            pltpu.VMEM((PAD, LANES), F32),
            pltpu.VMEM((PAD, LANES), F32),
            pltpu.VMEM((devices, kept_refs, capacity), BF),
            dma((held // ROWS,)),
            dma((n_blk,)), dma((n_blk,)), dma((n_blk,)), dma((n_blk,)),
            dma((n_blk,)), dma((n_blk,)),
            dma((devices,)), dma((devices,)),
            dma((half // COLS,)), dma((half // COLS,)),
            dma((half // COLS,)), dma((half // COLS,)),
            dma((n_blk // 2, half // COLS)), dma((n_blk // 2, half // COLS)),
            dma((n_blk,)), dma((n_blk,)),
            dma((2,)), dma((2,)),
        ],
        compiler_params=pltpu.CompilerParams(
            collective_id=0, has_side_effects=True, vmem_limit_bytes=60 << 20
        ),
        name="em_step",
    )(
        particles,
        defocus.reshape(1, held),
        pick_dest.reshape(1, held),
        references,
        ctf_table,
    )
    sums, weights, posterior = pl.pallas_call(
        finish,
        out_shape=(
            jax.ShapeDtypeStruct((rows_mine, pix), F32),
            jax.ShapeDtypeStruct((rows_mine, pix), F32),
            jax.ShapeDtypeStruct((kept_refs, devices * capacity), F32),
        ),
        in_specs=[vmem, vmem, vmem, vmem],
        out_specs=(vmem, vmem, vmem),
        compiler_params=pltpu.CompilerParams(vmem_limit_bytes=40 << 20),
        name="em_finish",
    )(sums, classes, ctf_table, posterior)
    return sums, weights, posterior.T


def solution(mesh):
    placed = (
        P(("groups", "blk", "dp"), None),
        P(("groups", "blk", "dp")),
        P(("groups", "blk", "dp"), None),
        P(("groups", "blk"), None),
        P("groups", None),
    )
    return jax.shard_map(
        per_device,
        mesh=mesh,
        in_specs=placed,
        out_specs=(
            P(("groups", "blk", "dp"), None),
            P(("groups", "blk", "dp"), None),
            P(("groups", "blk", "dp"), None),
        ),
        check_vma=False,
    )
```
